32 devices in a mesh: src: 4 (over z), rcv: 8 (over y, x, core).
Axes of the slice: x: 2, y: 2, z: 4, core: 2. Of those that a mesh axis runs over, the one named last changes fastest.
Arguments:
- traces: bfloat16 [16384, 2048], P(('src', 'rcv')), may hold values from -6 to 6
- trace_shot: int32 [16384], P(('src', 'rcv')), may hold values from 0 to 1023, as said below
- trace_receiver: int32 [16384], P(('src', 'rcv')), may hold values from 0 to 2047, as said below
- live: int32 [16384], P(('src', 'rcv')), may hold values 0 or 1
- window_start: int32 [16384], P(('src', 'rcv')), may hold values from 0 to 1536
- trace_owner: int32 [16384, 1], P(('src', 'rcv')), may hold values from 0 to 31; in each aligned block of 512 rows (0 to 511, 512 to 1023, ...) at most 24 rows name the same one
Outputs:
- regrouped: bfloat16 [24576, 2048], P(('src', 'rcv'))
- shot_terms: float32 [1024, 512], P('src')
- receiver_terms: float32 [2048, 512], P('rcv')
The draws below stay inside these ranges and needn't reach their ends.
Inputs may be any that keep to these rules, and one draw needn't show every extreme that they name: `trace_shot`: A trace in rows i * 4096 to (i + 1) * 4096 - 1 names one of the shots i * 256 to (i + 1) * 256 - 1. `trace_receiver`: A trace in rows of the device block b (rows b * 512 to (b + 1) * 512 - 1) names one of the receivers (b % (4096 // 512)) * 256 to that plus 256 - 1. `trace_owner`: among the 512 traces of one device at most 24 name the same owner; some owner is named exactly 24 times.
All inputs are finite; a program needn't handle non-finite values. No bound on the sum of `live` on one device may be relied on, other than what follows from the above.
Results may differ from the reference program's by a relative error of at most 0.009.
Values may be sent and summed in bfloat16 or wider, within the bound.
No kernel may reach another device: no remote copies, remote signals or barrier semaphores. Data moves between devices by JAX's collectives and lax.ppermute only.
A program may use at most 128 MiB of HBM per device.

```python
import math
import jax
import jax.numpy as jnp
import numpy as np
from jax import lax

W = 512
NS = 2048
TR_DEV = 512
SHOT_DEV = 256
RCV_DEV = 256
TRACES = 16384
TR_SRC = 4096
SHOTS = 1024
RECEIVERS = 2048
CAP = 24
N_SRC = 4
N_RCV = 8
DEVICES = 32


def draw_trace_shot(key, part):
    position = jnp.arange(TRACES, dtype=jnp.int32)
    group = position // TR_SRC
    offset = jax.random.randint(jax.random.fold_in(key, 11), (TRACES,), 0, SHOT_DEV, dtype=jnp.int32)
    return (group * SHOT_DEV + offset).astype(jnp.int32)


def draw_trace_receiver(key, part):
    position = jnp.arange(TRACES, dtype=jnp.int32)
    group = position // TR_DEV % (TR_SRC // TR_DEV)
    offset = jax.random.randint(jax.random.fold_in(key, 23), (TRACES,), 0, RCV_DEV, dtype=jnp.int32)
    return (group * RCV_DEV + offset).astype(jnp.int32)


def set_ends(values, key, low, top_value):
    index_at = [jax.random.randint(jax.random.fold_in(key, axis), (), 0, length) for axis, length in enumerate(values.shape)]
    longest = values.shape.index(max(values.shape))
    next_to = index_at[:longest] + [(index_at[longest] + 1) % values.shape[longest]] + index_at[longest + 1:]
    return values.at[tuple(index_at)].set(low).at[tuple(next_to)].set(top_value)


def levels(stream_key, extent, split, smallest, high):
    def one(axis_at, blocks):
        draws = jax.random.uniform(jax.random.fold_in(jax.random.fold_in(stream_key, 6), axis_at), (blocks,), jnp.float32, smallest / len(split), high / len(split))
        return jnp.repeat(jnp.exp(draws), extent[axis_at] // blocks).reshape((-1,) + (1,) * (len(extent) - axis_at - 1))

    gain = one(*split[0])
    for cut in split[1:]:
        gain = gain * one(*cut)
    return gain


def routed_block(stream_key, own, number, rows, count, top, reach, lean):
    ranking = jax.random.permutation(stream_key, count)
    crowded, ordinary = shares(count, rows * top, reach, lean, True), shares(count, rows * top, reach, lean, False)
    places = jnp.arange(count)

    def named(lengths, offset_by):
        used = int((lengths > 0).sum())
        fixed = max(1, used // 4)
        passed = fixed + (places - fixed + offset_by * (used - fixed)) % max(1, count - fixed)
        return jnp.zeros((count,), jnp.int32).at[ranking[jnp.where(places < fixed, places, passed)]].set(jnp.asarray(lengths, jnp.int32))

    lengths = jnp.where(number % 4 == 0, named(crowded, number // 4), named(ordinary, number - number // 4 - 1))
    mixed = jax.random.permutation(jax.random.fold_in(own, 3), count)
    source_of, taker = mixed[0:count // 2 * 2:2], mixed[1:count // 2 * 2:2]
    room = jnp.minimum(lengths[source_of] - 1, reach - lengths[taker]) // 2
    room = jnp.where((source_of == ranking[0]) | (taker == ranking[0]) | (lengths[taker] == 0), 0, jnp.maximum(room, 0))
    passed = jax.random.randint(jax.random.fold_in(own, 4), (count // 2,), 0, 1 << 20) % (room + 1)
    lengths = lengths.at[source_of].add(-passed).at[taker].add(passed)
    members = jnp.searchsorted(jnp.cumsum(lengths), jnp.arange(rows * top), side="right").astype(jnp.int32)
    listing = members.reshape(top, rows).T
    listing = listing[jax.random.permutation(jax.random.fold_in(own, 1), rows)]
    offset_by = jax.random.randint(jax.random.fold_in(own, 2), (rows, 1), 0, top)
    return jnp.take_along_axis(listing, (jnp.arange(top)[None, :] + offset_by) % top, axis=1)


def shares(amount, total, bound, skew, full):
    loads = [(1 << 20) // math.isqrt(grade ** skew) + 1 for grade in range(1, amount + 1)]
    largest = bound if full else min(bound, max(-(-total // amount), total * loads[0] // sum(loads)))
    least = 1 if total - largest >= amount - 1 else 0
    given, surplus = [largest] + [least] * (amount - 1), total - largest - least * (amount - 1)
    while surplus > 0:
        movable = [i for i in range(1, amount) if given[i] < largest] or [i for i in range(1, amount) if given[i] < bound]
        mass, budget = sum([loads[i] for i in movable]), surplus
        for i in movable:
            more = min(bound - given[i], max(1, budget * loads[i] // mass), surplus)
            given[i] = given[i] + more
            surplus = surplus - more
    return np.array(given)


def centred(own_key, shape, scale, bound, cuts=(), kind=jnp.bfloat16):
    drawn = jax.random.normal(own_key, shape, jnp.float32) * scale
    if len(cuts) > 0:
        drawn = levels(own_key, shape, cuts, -0.22, 0.18) * drawn
    return jnp.clip(drawn, min=-bound, max=bound).astype(kind)


def setup_inputs(seed: int = 0) -> dict:
    key_of = jax.random.split(jax.random.key(seed), 7)
    traces = centred(key_of[0], (TRACES, NS), 1.0, 6.0, ((0, 32),))
    trace_shot = draw_trace_shot(jax.random.fold_in(key_of[6], 71), 0)
    trace_receiver = draw_trace_receiver(jax.random.fold_in(key_of[6], 71), 0)
    live = set_ends((jax.random.randint(key_of[3], (TRACES,), 0, 4) < 3).astype(jnp.int32), jax.random.fold_in(key_of[3], 1), 0, 1)
    window_start = set_ends(jax.random.randint(key_of[4], (TRACES,), 0, NS - W + 1), jax.random.fold_in(key_of[4], 1), 0, NS - W).astype(jnp.int32)
    trace_owner_keys = jax.random.split(jax.random.fold_in(key_of[5], 1), TRACES // TR_DEV)
    trace_owner_turns = jax.random.permutation(jax.random.fold_in(key_of[5], 3), TRACES // TR_DEV)
    trace_owner = jax.vmap(lambda own, number: routed_block(jax.random.fold_in(key_of[5], 2), own, number, TR_DEV, DEVICES, 1, CAP, 2))(trace_owner_keys, trace_owner_turns).reshape((TRACES, 1))
    return dict(traces=traces, trace_shot=trace_shot, trace_receiver=trace_receiver, live=live, window_start=window_start, trace_owner=trace_owner)


def phases(length):
    position = jnp.arange(length, dtype=jnp.int32)
    product = position[:, None] * position[None, :] % length
    return 2.0 * math.pi / length * product.astype(jnp.float32)

def tables(length, stride):
    angle = phases(length)
    cosine = jnp.cos(angle)
    sine = jnp.sin(angle)
    position = jnp.arange(length, dtype=jnp.int32)
    taper = 0.5 - 0.5 * jnp.cos(2.0 * math.pi / length * position.astype(jnp.float32))
    full = jnp.concatenate([cosine, -sine], 1)
    analysis = (full * (taper / math.sqrt(length))[:, None]).astype(jnp.bfloat16)
    forward = full[:stride].astype(jnp.bfloat16)
    inverse = (jnp.concatenate([cosine, -sine], 0) / length).astype(jnp.bfloat16)
    half = length // 2
    folding = jnp.where((position == 0) | (position == half), 1.0, jnp.where(position < half, 2.0, 0.0)).astype(jnp.float32)
    kernel = jnp.dot(cosine / length, folding[:, None] * full, precision=lax.Precision.HIGHEST)
    return (analysis, forward, inverse, kernel)

def exact_dot(left, right):
    return jnp.dot(left.astype(jnp.float32), right.astype(jnp.float32), precision=lax.Precision.HIGHEST)

def filter_block(block_traces, gain_real, gain_imag, forward, inverse, stride):
    rows, samples = block_traces.shape
    pieces = samples // stride
    length = inverse.shape[1]
    spectra = exact_dot(block_traces.reshape(rows * pieces, stride), forward).reshape(rows, pieces, 2 * length)
    real_part = spectra[..., :length]
    imag_part = spectra[..., length:]
    out_real = real_part * gain_real[:, None, :] - imag_part * gain_imag[:, None, :]
    out_imag = real_part * gain_imag[:, None, :] + imag_part * gain_real[:, None, :]
    product = jnp.concatenate([out_real, out_imag], -1).astype(jnp.bfloat16).reshape(rows * pieces, 2 * length)
    series = exact_dot(product, inverse).reshape(rows, pieces, length)
    leading = series[..., :stride]
    carried = jnp.concatenate([jnp.zeros((rows, 1, stride), jnp.float32), series[:, :-1, stride:]], 1)
    return (leading + carried).reshape(rows, samples).astype(jnp.bfloat16)

def reference(traces, trace_shot, trace_receiver, live, window_start, trace_owner):
    stride = W // 2
    devices = N_SRC * N_RCV
    analysis, forward, inverse, kernel = tables(W, stride)
    spots = window_start[:, None] + jnp.arange(W, dtype=jnp.int32)[None, :]
    windows = jnp.take_along_axis(traces, spots, 1)
    spectra = exact_dot(windows, analysis)
    power = spectra[:, :W] ** 2 + spectra[:, W:] ** 2
    logs = 0.5 * jnp.log(power + 0.01 * lax.optimization_barrier(jnp.mean(power, 1, keepdims=True)) + 1e-06)
    weight = live.astype(jnp.float32)
    shot_count = jax.ops.segment_sum(weight, trace_shot, SHOTS)
    receiver_count = jax.ops.segment_sum(weight, trace_receiver, RECEIVERS)
    weighted = weight[:, None] * logs
    shot_first = jax.ops.segment_sum(weighted, trace_shot, SHOTS) / (1.0 + shot_count)[:, None]
    receiver_first = jax.ops.segment_sum(weighted, trace_receiver, RECEIVERS) / (1.0 + receiver_count)[:, None]
    shot_terms = jax.ops.segment_sum(weight[:, None] * (logs - receiver_first[trace_receiver]), trace_shot, SHOTS) / (1.0 + shot_count)[:, None]
    receiver_terms = jax.ops.segment_sum(weight[:, None] * (logs - shot_first[trace_shot]), trace_receiver, RECEIVERS) / (1.0 + receiver_count)[:, None]
    shot_spectra = jnp.dot(shot_terms, kernel, precision=lax.Precision.HIGHEST)
    receiver_spectra = jnp.dot(receiver_terms, kernel, precision=lax.Precision.HIGHEST)

    def one_device(items):
        block_traces, shots_here, receivers_here = items
        log_gain = -(shot_spectra[shots_here] + receiver_spectra[receivers_here])
        magnitude = jnp.exp(log_gain[:, :W])
        gain_real = magnitude * jnp.cos(log_gain[:, W:])
        gain_imag = magnitude * jnp.sin(log_gain[:, W:])
        return filter_block(block_traces, gain_real, gain_imag, forward, inverse, stride)
    filtered = lax.map(one_device, (traces.reshape(devices, TR_DEV, NS), trace_shot.reshape(devices, TR_DEV), trace_receiver.reshape(devices, TR_DEV)))
    filtered = filtered.reshape(devices * TR_DEV, NS)
    owner = trace_owner[:, 0]
    owner_blocks = owner.reshape(devices, TR_DEV)
    hot = (owner_blocks[:, :, None] == jnp.arange(devices, dtype=jnp.int32)[None, None, :]).astype(jnp.int32)
    ranks = jnp.cumsum(hot, 1) - hot
    slot = lax.optimization_barrier(jnp.sum(ranks * hot, -1)).reshape(devices * TR_DEV)
    source = (jnp.arange(devices * TR_DEV, dtype=jnp.int32) // TR_DEV).astype(jnp.int32)
    target = owner * (devices * CAP) + source * CAP + slot
    regrouped = jnp.zeros((devices * devices * CAP, NS), jnp.bfloat16).at[target].set(filtered)
    return (regrouped, shot_terms, receiver_terms)
```

```python
import functools
import math

import jax
import jax.numpy as jnp
import numpy as np
from jax import lax
from jax.experimental import pallas as pl
from jax.experimental.pallas import tpu as pltpu
from jax.sharding import PartitionSpec as P

W = 512
HALF = W // 2
WIDE = HALF + 128
AUX = 16
STATIONS = 256
DAMPING = 1.0
F32 = jnp.float32
BF16 = jnp.bfloat16


def split_table(table):
    high = table.astype(np.float32).astype(jnp.bfloat16)
    low = (table - high.astype(np.float64)).astype(np.float32).astype(jnp.bfloat16)
    return high, low


@functools.cache
def tables():
    index = np.arange(W)
    angle = 2.0 * np.pi / W * (index[:, None] * index[None, :] % W)
    cosine, sine = np.cos(angle), np.sin(angle)
    nyquist = np.where(index % 2 == 0, 1.0, -1.0)
    packed = np.concatenate([cosine[:, :HALF], -sine[:, :HALF]], 1)
    packed[:, HALF] = nyquist
    analysis = split_table(packed)
    forward = packed[:HALF].astype(np.float32).astype(jnp.bfloat16)
    weight = np.full((W, 1), 2.0)
    weight[0] = weight[HALF] = 1.0
    inverse = (packed.T * weight / W).astype(np.float32).astype(jnp.bfloat16)
    fold = np.where((index == 0) | (index == HALF), 1.0, np.where(index < HALF, 2.0, 0.0))
    full = (cosine / W) @ (fold[:, None] * -sine)
    hilbert = np.zeros((WIDE, HALF))
    hilbert[: HALF + 1] = full[: HALF + 1, :HALF]
    hilbert[1:HALF] += full[:HALF:-1, :HALF]
    hilbert[:, 0] = 0.0
    return analysis, forward, inverse, split_table(hilbert)


def dot(left, right):
    return jnp.dot(left, right, preferred_element_type=F32)


def halves(value):
    high = value.astype(BF16)
    return high, (value - high.astype(F32)).astype(BF16)


def select_rows(hot, value):
    high, low = halves(value)
    return dot(hot, high) + dot(hot, low)


def column(row):
    return jnp.concatenate(
        [
            jnp.transpose(jnp.broadcast_to(row[:, at : at + 128], (128, 128)))
            for at in range(0, row.shape[1], 128)
        ],
        0,
    )


def tile_lanes(value, width):
    return jnp.concatenate([value] * (width // value.shape[1]), 1)


def hot_columns(row):
    station = lax.broadcasted_iota(jnp.int32, (STATIONS, row.shape[1]), 0)
    return station == row


def hot_rows(row):
    station = lax.broadcasted_iota(jnp.int32, (row.shape[1], STATIONS), 1)
    return (station == tile_lanes(column(row), STATIONS)).astype(F32).astype(BF16)


def aux_rows(*rows):
    at = lax.broadcasted_iota(jnp.int32, (AUX, STATIONS), 0)
    out = jnp.zeros((AUX, STATIONS), F32)
    for number, row in enumerate(rows):
        out = jnp.where(at == number, row, out)
    return out


def put_sums(out, sums, counted):
    flipped = jnp.transpose(sums[:, HALF:])
    rows = [flipped[:1]]
    if counted:
        count = flipped[1:2]
        top = jnp.floor(count * (1 / 256))
        rest = count - 256.0 * top
        middle = jnp.floor(rest * (1 / 16))
        rows += [rest - 16.0 * middle, middle, top]
    out[:STATIONS, :] = sums[:, :HALF].astype(BF16)
    out[STATIONS:, :] = aux_rows(*rows).astype(BF16)


def get_sums(own, other):
    main = own[:STATIONS, :].astype(F32) + other[:STATIONS, :].astype(F32)
    aux = own[STATIONS:, :].astype(F32) + other[STATIONS:, :].astype(F32)
    aux = jnp.concatenate([aux, jnp.zeros((128 - AUX, STATIONS), F32)], 0)
    return main, jnp.transpose(aux)


def counts_of(aux):
    return DAMPING + (aux[:, 1:2] + 16.0 * aux[:, 2:3] + 256.0 * aux[:, 3:4])


def join(main, aux):
    lane = lax.broadcasted_iota(jnp.int32, aux.shape, 1)
    return jnp.concatenate([main, jnp.where(lane == 0, aux, 0.0)], 1)


def logs_kernel(capacity, owners, meta, traces, high, low, logs, shots, receivers, target):
    step = pl.program_id(0)
    rows, samples = traces.shape
    here = meta[:, pl.ds(pl.multiple_of(step * rows, rows), rows)]
    start = here[3:4]
    offset = start % W
    phase = (2.0 * math.pi / W) * offset.astype(F32)
    offset_col = tile_lanes(column(offset), W)
    block_col = tile_lanes(column(start // W), W)
    cos_col = tile_lanes(column(jnp.cos(phase)), W)
    sin_col = tile_lanes(column(jnp.sin(phase)), W)
    lane = lax.broadcasted_iota(jnp.int32, (rows, W), 1)
    lane_phase = (2.0 * math.pi / W) * lax.broadcasted_iota(jnp.int32, (8, W), 1).astype(F32)
    lane_cos = jnp.cos(lane_phase)[:1]
    lane_sin = jnp.sin(lane_phase)[:1]
    block = block_col + (lane < offset_col).astype(jnp.int32)
    folded = traces[:, :W].astype(F32)
    for at in range(1, samples // W):
        folded = jnp.where(block == at, traces[:, at * W : (at + 1) * W].astype(F32), folded)
    tapered = folded * (0.5 - 0.5 * (lane_cos * cos_col + lane_sin * sin_col))
    first, second = halves(tapered)
    spectra = dot(first, high[...]) + dot(second, high[...]) + dot(first, low[...])
    real, imag = spectra[:, :HALF], spectra[:, HALF:]
    lane = lax.broadcasted_iota(jnp.int32, (rows, HALF), 1)
    nyquist = imag[:, :1] * imag[:, :1]
    power = real * real + jnp.where(lane == 0, 0.0, imag * imag)
    total = 2.0 * jnp.sum(power, 1, keepdims=True) - power[:, :1] + nyquist
    floor = total * (0.01 / W / W) + 1e-6
    at = pl.ds(pl.multiple_of(step * rows, rows), rows)
    logs[at, :HALF] = 0.5 * jnp.log(power * (1 / W) + floor)
    lane = lax.broadcasted_iota(jnp.int32, (rows, 128), 1)
    last = 0.5 * jnp.log(nyquist * (1 / W) + floor)
    logs[at, HALF:] = jnp.where(lane == 0, last, jnp.where(lane == 1, 1.0, 0.0))

    @pl.when(step == pl.num_programs(0) - 1)
    def _():
        live = meta[2:3, :].astype(F32)
        first, second = halves(logs[...])
        for number, out in ((0, shots), (1, receivers)):
            hot = jnp.where(hot_columns(meta[number : number + 1, :]), live, 0.0).astype(BF16)
            put_sums(out, dot(hot, first) + dot(hot, second), True)
        owner = meta[4:5, :]
        total_rows = owner.shape[1]
        device = lax.broadcasted_iota(jnp.int32, (owners, total_rows), 0)
        hot = jnp.where(device == owner, 1.0, 0.0)
        before = lax.broadcasted_iota(jnp.int32, (total_rows, total_rows), 0)
        after = lax.broadcasted_iota(jnp.int32, (total_rows, total_rows), 1)
        earlier = jnp.where(before < after, 1.0, 0.0).astype(BF16)
        slot = jnp.sum(dot(hot.astype(BF16), earlier) * hot, 0, keepdims=True)
        target[...] = jnp.broadcast_to(owner * capacity + slot.astype(jnp.int32), target.shape)


def second_kernel(meta, logs, shots, shots_in, receivers, receivers_in, shots_out, receivers_out):
    live = meta[2:3, :].astype(F32)
    rows = [meta[0:1, :], meta[1:2, :]]
    values = logs[...]
    firsts = []
    for own, other in ((shots, shots_in), (receivers, receivers_in)):
        main, aux = get_sums(own, other)
        firsts.append(join(main, aux) / counts_of(aux))
    for number, out in ((0, shots_out), (1, receivers_out)):
        other = 1 - number
        rest = values - select_rows(hot_rows(rows[other]), firsts[other])
        hot = jnp.where(hot_columns(rows[number]), live, 0.0).astype(BF16)
        put_sums(out, select_rows(hot, rest), False)


def terms_of(own, other, first, first_in):
    main, aux = get_sums(own, other)
    _, aux_first = get_sums(first, first_in)
    return join(main, aux) / counts_of(aux_first)


def terms_kernel(shots, shots_in, receivers, receivers_in, a, a_in, b, b_in, shot_out, receiver_out):
    row = lax.broadcasted_iota(jnp.int32, (HALF, HALF), 0)
    lane = lax.broadcasted_iota(jnp.int32, (HALF, HALF), 1)
    turned = jnp.where(row + lane == HALF, 1.0, 0.0).astype(BF16)
    for out, parts in (
        (shot_out, (shots, shots_in, a, a_in)),
        (receiver_out, (receivers, receivers_in, b, b_in)),
    ):
        terms = terms_of(*parts)
        main = terms[:, :HALF]
        out[:, :HALF] = main
        high, rest = main.astype(BF16), 0.0
        rest = main - high.astype(F32)
        middle = rest.astype(BF16)
        low = (rest - middle.astype(F32)).astype(BF16)
        mirror = dot(high, turned) + dot(middle, turned) + dot(low, turned)
        out[:, HALF:] = jnp.where(lane == 0, terms[:, HALF : HALF + 1], mirror)


def sin_cos(angle):
    turns = jnp.floor(angle * (2.0 / math.pi) + 0.5)
    rest = angle - turns * 1.5707855224609375
    rest = rest - turns * 1.0804334124e-05
    square = rest * rest
    sine = rest + rest * square * (
        -1.6666654611e-1 + square * (8.3321608736e-3 - square * 1.9515295891e-4)
    )
    cosine = 1.0 - 0.5 * square + square * square * (
        4.166664568298827e-2 + square * (-1.388731625493765e-3 + square * 2.443315711809948e-5)
    )
    quarter = turns.astype(jnp.int32) & 3
    odd = (quarter & 1) == 1
    sin_out = jnp.where(odd, cosine, sine)
    cos_out = jnp.where(odd, sine, cosine)
    sin_out = jnp.where(quarter >= 2, -sin_out, sin_out)
    cos_out = jnp.where((quarter == 1) | (quarter == 2), -cos_out, cos_out)
    return sin_out, cos_out


def filter_kernel(
    meta, target, shots, shots_in, receivers, receivers_in, a, a_in, b, b_in,
    hilbert_high, hilbert_low, forward, inverse, traces, out,
    gain_real, gain_imag, gain_last, placing, before,
):
    @pl.when(pl.program_id(0) == 0)
    def _():
        shot_terms = terms_of(shots, shots_in, a, a_in)
        receiver_terms = terms_of(receivers, receivers_in, b, b_in)
        level = -(
            select_rows(hot_rows(meta[0:1, :]), shot_terms)
            + select_rows(hot_rows(meta[1:2, :]), receiver_terms)
        )
        first, second = halves(level)
        angle = (
            dot(first, hilbert_high[...])
            + dot(second, hilbert_high[...])
            + dot(first, hilbert_low[...])
        )
        size = jnp.exp(level)
        sine, cosine = sin_cos(angle)
        main = size[:, :HALF]
        real = main * cosine
        lane = lax.broadcasted_iota(jnp.int32, real.shape, 1)
        gain_real[...] = real
        gain_imag[...] = main * sine
        gain_last[...] = jnp.where(lane == 0, size[:, HALF : HALF + 1], real)
        row = lax.broadcasted_iota(jnp.int32, placing.shape, 0)
        placing[...] = jnp.where(row == target[:1, :], 1.0, 0.0).astype(BF16)
        before[...] = jnp.zeros_like(before)

    spectra = dot(traces[...], forward[...])
    real, imag = spectra[:, :HALF], spectra[:, HALF:]
    product = jnp.concatenate(
        [
            (real * gain_real[...] - imag * gain_imag[...]).astype(BF16),
            (real * gain_imag[...] + imag * gain_last[...]).astype(BF16),
        ],
        1,
    )
    series = dot(product, inverse[...])
    filtered = (series[:, :HALF] + before[...]).astype(BF16)
    before[...] = series[:, HALF:]
    out[...] = dot(placing[...], filtered).astype(BF16)


def whole(shape):
    return pl.BlockSpec(shape, lambda *_: (0,) * len(shape))


def butterfly(value, name):
    size = lax.axis_size(name)
    other = jnp.zeros_like(value)
    bit = 1
    while bit < size:
        if bit > 1:
            value = (value.astype(F32) + other.astype(F32)).astype(BF16)
        other = lax.ppermute(value, name, [(i, i ^ bit) for i in range(size)])
        bit *= 2
    return value, other


def on_device(traces, trace_shot, trace_receiver, live, window_start, trace_owner):
    rows, samples = traces.shape
    devices = lax.axis_size("src") * lax.axis_size("rcv")
    capacity = max(2, 3 * rows // (2 * devices))
    (high, low), forward, inverse, (hilbert_high, hilbert_low) = tables()
    zero = jnp.zeros_like(live)
    meta = jnp.stack(
        [
            trace_shot - lax.axis_index("src") * STATIONS,
            trace_receiver - lax.axis_index("rcv") * STATIONS,
            live,
            window_start,
            trace_owner[:, 0],
            zero,
            zero,
            zero,
        ]
    )
    packed = jax.ShapeDtypeStruct((STATIONS + AUX, HALF), BF16)
    block = min(128, rows)
    owners = max(16, devices)
    logs, shots, receivers, target = pl.pallas_call(
        functools.partial(logs_kernel, capacity, owners),
        grid=(rows // block,),
        in_specs=[
            whole((8, rows)),
            pl.BlockSpec((block, samples), lambda i: (i, 0)),
            whole((W, W)),
            whole((W, W)),
        ],
        out_specs=[
            whole((rows, WIDE)),
            whole(packed.shape),
            whole(packed.shape),
            whole((8, rows)),
        ],
        out_shape=[
            jax.ShapeDtypeStruct((rows, WIDE), F32),
            packed,
            packed,
            jax.ShapeDtypeStruct((8, rows), jnp.int32),
        ],
        name="logs",
    )(meta, traces, high, low)
    shots, shots_in = butterfly(shots, "rcv")
    receivers, receivers_in = butterfly(receivers, "src")
    firsts = (shots, shots_in, receivers, receivers_in)
    a, b = pl.pallas_call(second_kernel, out_shape=[packed, packed], name="second")(
        meta, logs, *firsts
    )
    a, a_in = butterfly(a, "rcv")
    b, b_in = butterfly(b, "src")
    sums = (a, a_in, b, b_in) + firsts
    outgoing = pl.pallas_call(
        filter_kernel,
        grid=(samples // HALF,),
        in_specs=[whole((8, rows)), whole((8, rows))]
        + [whole(packed.shape)] * 8
        + [whole((WIDE, HALF)), whole((WIDE, HALF)), whole((HALF, W)), whole((W, W))]
        + [pl.BlockSpec((rows, HALF), lambda j: (0, j))],
        out_specs=pl.BlockSpec((devices * capacity, HALF), lambda j: (0, j)),
        out_shape=jax.ShapeDtypeStruct((devices * capacity, samples), BF16),
        scratch_shapes=[pltpu.VMEM((rows, HALF), F32)] * 3
        + [pltpu.VMEM((devices * capacity, rows), BF16), pltpu.VMEM((rows, HALF), F32)],
        name="filter",
    )(meta, target, *sums, hilbert_high, hilbert_low, forward, inverse, traces)
    regrouped = lax.all_to_all(outgoing, ("src", "rcv"), split_axis=0, concat_axis=0, tiled=True)
    terms = jax.ShapeDtypeStruct((STATIONS, W), F32)
    shot_terms, receiver_terms = pl.pallas_call(
        terms_kernel, out_shape=[terms, terms], name="terms"
    )(*sums)
    return (regrouped, shot_terms, receiver_terms)


def solution(mesh):
    return jax.shard_map(
        on_device,
        mesh=mesh,
        in_specs=(
            P(("src", "rcv"), None),
            P(("src", "rcv")),
            P(("src", "rcv")),
            P(("src", "rcv")),
            P(("src", "rcv")),
            P(("src", "rcv"), None),
        ),
        out_specs=(P(("src", "rcv"), None), P("src", None), P("rcv", None)),
        check_vma=False,
    )
```

```python
import functools
import math

import jax
import jax.numpy as jnp
import numpy as np
from jax import lax
from jax.experimental import pallas as pl
from jax.experimental.pallas import tpu as pltpu
from jax.sharding import PartitionSpec as P

W = 512
HALF = W // 2
WIDE = HALF + 128
AUX = 16
STATIONS = 256
DAMPING = 1.0
VMEM_LIMIT = 20 * 2**20
SPAN = 2
SHARES = (3, 4, 5)
PARTS = len(SHARES)
F32 = jnp.float32
BF16 = jnp.bfloat16


def split_table(table):
    high = table.astype(np.float32).astype(jnp.bfloat16)
    low = (table - high.astype(np.float64)).astype(np.float32).astype(jnp.bfloat16)
    return high, low


@functools.cache
def tables():
    index = np.arange(W)
    angle = 2.0 * np.pi / W * (index[:, None] * index[None, :] % W)
    cosine, sine = np.cos(angle), np.sin(angle)
    nyquist = np.where(index % 2 == 0, 1.0, -1.0)
    packed = np.concatenate([cosine[:, :HALF], -sine[:, :HALF]], 1)
    packed[:, HALF] = nyquist
    analysis = split_table(packed)
    forward = packed[:HALF].astype(np.float32).astype(jnp.bfloat16)
    weight = np.full((W, 1), 2.0)
    weight[0] = weight[HALF] = 1.0
    inverse = (packed.T * weight / W).astype(np.float32).astype(jnp.bfloat16)
    fold = np.where((index == 0) | (index == HALF), 1.0, np.where(index < HALF, 2.0, 0.0))
    full = (cosine / W) @ (fold[:, None] * -sine)
    hilbert = np.zeros((WIDE, HALF))
    hilbert[: HALF + 1] = full[: HALF + 1, :HALF]
    hilbert[1:HALF] += full[:HALF:-1, :HALF]
    hilbert[:, 0] = 0.0
    return analysis, forward, inverse, split_table(hilbert)


def dot(left, right):
    return jnp.dot(left, right, preferred_element_type=F32)


def halves(value):
    high = value.astype(BF16)
    return high, (value - high.astype(F32)).astype(BF16)


def select_rows(hot, value):
    high, low = halves(value)
    return dot(hot, high) + dot(hot, low)


def column(row):
    return jnp.concatenate(
        [
            jnp.transpose(jnp.broadcast_to(row[:, at : at + 128], (128, 128)))
            for at in range(0, row.shape[1], 128)
        ],
        0,
    )


def tile_lanes(value, width):
    return jnp.concatenate([value] * (width // value.shape[1]), 1)


def pad_lanes(size):
    return -(-size // 128) * 128


def hot_columns(row):
    station = lax.broadcasted_iota(jnp.int32, (STATIONS, row.shape[1]), 0)
    return station == row


def hot_rows(row):
    station = lax.broadcasted_iota(jnp.int32, (row.shape[1], STATIONS), 1)
    return (station == tile_lanes(column(row), STATIONS)).astype(F32).astype(BF16)


def aux_rows(*rows):
    at = lax.broadcasted_iota(jnp.int32, (AUX, STATIONS), 0)
    out = jnp.zeros((AUX, STATIONS), F32)
    for number, row in enumerate(rows):
        out = jnp.where(at == number, row, out)
    return out


def put_sums(out, sums, counted):
    flipped = jnp.transpose(sums[:, HALF:])
    rows = [flipped[:1]]
    if counted:
        count = flipped[1:2]
        top = jnp.floor(count * (1 / 256))
        rest = count - 256.0 * top
        middle = jnp.floor(rest * (1 / 16))
        rows += [rest - 16.0 * middle, middle, top]
    out[:STATIONS, :] = sums[:, :HALF].astype(BF16)
    out[STATIONS:, :] = aux_rows(*rows).astype(BF16)


def get_sums(own, other):
    main = own[:STATIONS, :].astype(F32) + other[:STATIONS, :].astype(F32)
    aux = own[STATIONS:, :].astype(F32) + other[STATIONS:, :].astype(F32)
    aux = jnp.concatenate([aux, jnp.zeros((128 - AUX, STATIONS), F32)], 0)
    return main, jnp.transpose(aux)


def counts_of(aux):
    return DAMPING + (aux[:, 1:2] + 16.0 * aux[:, 2:3] + 256.0 * aux[:, 3:4])


def join(main, aux):
    lane = lax.broadcasted_iota(jnp.int32, aux.shape, 1)
    return jnp.concatenate([main, jnp.where(lane == 0, aux, 0.0)], 1)


def station_rows(shot, receiver):
    shot_row = shot[...] - lax.axis_index("src") * STATIONS
    return shot_row, receiver[...] - lax.axis_index("rcv") * STATIONS


def logs_kernel(shot, receiver, live, start_row, traces, high, low, logs, shots, receivers):
    step = pl.program_id(0)
    rows, samples = traces.shape
    start = start_row[:, pl.ds(pl.multiple_of(step * rows, rows), rows)]
    offset = start % W
    phase = (2.0 * math.pi / W) * offset.astype(F32)
    offset_col = tile_lanes(column(offset), W)
    block_col = tile_lanes(column(start // W), W)
    cos_col = tile_lanes(column(jnp.cos(phase)), W)
    sin_col = tile_lanes(column(jnp.sin(phase)), W)
    lane = lax.broadcasted_iota(jnp.int32, (rows, W), 1)
    lane_phase = (2.0 * math.pi / W) * lax.broadcasted_iota(jnp.int32, (8, W), 1).astype(F32)
    lane_cos = jnp.cos(lane_phase)[:1]
    lane_sin = jnp.sin(lane_phase)[:1]
    block = block_col + (lane < offset_col).astype(jnp.int32)
    folded = traces[:, :W].astype(F32)
    for at in range(1, samples // W):
        folded = jnp.where(block == at, traces[:, at * W : (at + 1) * W].astype(F32), folded)
    tapered = folded * (0.5 - 0.5 * (lane_cos * cos_col + lane_sin * sin_col))
    first, second = halves(tapered)
    spectra = dot(first, high[...]) + dot(second, high[...]) + dot(first, low[...])
    real, imag = spectra[:, :HALF], spectra[:, HALF:]
    lane = lax.broadcasted_iota(jnp.int32, (rows, HALF), 1)
    nyquist = imag[:, :1] * imag[:, :1]
    power = real * real + jnp.where(lane == 0, 0.0, imag * imag)
    total = 2.0 * jnp.sum(power, 1, keepdims=True) - power[:, :1] + nyquist
    floor = total * (0.01 / W / W) + 1e-6
    at = pl.ds(pl.multiple_of(step * rows, rows), rows)
    logs[at, :HALF] = 0.5 * jnp.log(power * (1 / W) + floor)
    lane = lax.broadcasted_iota(jnp.int32, (rows, 128), 1)
    last = 0.5 * jnp.log(nyquist * (1 / W) + floor)
    logs[at, HALF:] = jnp.where(lane == 0, last, jnp.where(lane == 1, 1.0, 0.0))

    @pl.when(step == pl.num_programs(0) - 1)
    def _():
        weight = live[...].astype(F32)
        first, second = halves(logs[...])
        for row, out in zip(station_rows(shot, receiver), (shots, receivers)):
            hot = jnp.where(hot_columns(row), weight, 0.0).astype(BF16)
            put_sums(out, dot(hot, first) + dot(hot, second), True)


def second_kernel(
    shot, receiver, live, logs, shots, shots_in, receivers, receivers_in, shots_out, receivers_out
):
    weight = live[...].astype(F32)
    rows = station_rows(shot, receiver)
    values = logs[...]
    firsts = []
    for own, other in ((shots, shots_in), (receivers, receivers_in)):
        main, aux = get_sums(own, other)
        firsts.append(join(main, aux) / counts_of(aux))
    for number, out in ((0, shots_out), (1, receivers_out)):
        other = 1 - number
        rest = values - select_rows(hot_rows(rows[other]), firsts[other])
        hot = jnp.where(hot_columns(rows[number]), weight, 0.0).astype(BF16)
        put_sums(out, select_rows(hot, rest), False)


def terms_of(own, other, first, first_in):
    main, aux = get_sums(own, other)
    _, aux_first = get_sums(first, first_in)
    return join(main, aux) / counts_of(aux_first)


def terms_kernel(shots, shots_in, receivers, receivers_in, a, a_in, b, b_in, shot_out, receiver_out):
    row = lax.broadcasted_iota(jnp.int32, (HALF, HALF), 0)
    lane = lax.broadcasted_iota(jnp.int32, (HALF, HALF), 1)
    turned = jnp.where(row + lane == HALF, 1.0, 0.0).astype(BF16)
    for out, parts in (
        (shot_out, (shots, shots_in, a, a_in)),
        (receiver_out, (receivers, receivers_in, b, b_in)),
    ):
        terms = terms_of(*parts)
        main = terms[:, :HALF]
        out[:, :HALF] = main
        high, rest = main.astype(BF16), 0.0
        rest = main - high.astype(F32)
        middle = rest.astype(BF16)
        low = (rest - middle.astype(F32)).astype(BF16)
        mirror = dot(high, turned) + dot(middle, turned) + dot(low, turned)
        out[:, HALF:] = jnp.where(lane == 0, terms[:, HALF : HALF + 1], mirror)


def sin_cos(angle):
    turns = jnp.floor(angle * (0.5 / math.pi) + 0.5)
    rest = (angle - turns * 6.28125) - turns * 1.9353071795864769e-3
    rest = rest * 0.25
    square = rest * rest
    sine = rest + rest * square * (
        -1.6666654611e-1 + square * (8.3321608736e-3 - square * 1.9515295891e-4)
    )
    short = square * (
        0.5 - square * (4.166664568298827e-2 - square * (1.388731625493765e-3 - square * 2.443315711809948e-5))
    )
    for _ in range(2):
        sine, short = 2.0 * sine * (1.0 - short), 2.0 * sine * sine
    return sine, 1.0 - short


def place_kernel(
    sides, capacity, shot, receiver, owner, traces, *rest
):
    src, rcv = sides
    plane, early = rcv * capacity, src - 2
    own, parts = rest[0], rest[1:-4]
    own_shot, own_receiver, early_index, placing = rest[-4:]

    @pl.when(pl.program_id(0) == 0)
    def _():
        owners = owner[...]
        rows = owners.shape[1]
        device = lax.broadcasted_iota(jnp.int32, (max(16, src * rcv), rows), 0)
        hot = jnp.where(device == owners, 1.0, 0.0)
        before = lax.broadcasted_iota(jnp.int32, (rows, rows), 0)
        after = lax.broadcasted_iota(jnp.int32, (rows, rows), 1)
        earlier = jnp.where(before < after, 1.0, 0.0).astype(BF16)
        slot = jnp.sum(dot(hot.astype(BF16), earlier) * hot, 0, keepdims=True).astype(jnp.int32)
        top, side = owners // rcv, owners % rcv
        mask = top ^ lax.axis_index("src")
        late = (top // (src // 2)) * plane + side * capacity
        number = jnp.where(mask < src // 2, mask + 1, mask)
        relayed = number * plane + (side ^ lax.axis_index("rcv")) * capacity
        target = jnp.where(mask % (src // 2) == 0, late, relayed) + slot
        row = lax.broadcasted_iota(jnp.int32, placing.shape, 0)
        placing[...] = jnp.where(row == target, 1.0, 0.0).astype(BF16)
        shot_row, receiver_row = station_rows(shot, receiver)
        at = lax.broadcasted_iota(jnp.int32, (AUX, rows), 0)
        stations = jnp.where(at == 0, shot_row, jnp.where(at == 1, receiver_row, 0))
        stations = stations.astype(F32).astype(BF16)

        def find(first, size):
            return lax.dot_general(
                stations,
                placing[first : first + size, :],
                (((1,), (1,)), ((), ())),
                preferred_element_type=F32,
            )

        found = find(0, own_shot.shape[0])
        own_shot[...] = hot_rows(found[:1].astype(jnp.int32))
        own_receiver[...] = hot_rows(found[1:2].astype(jnp.int32))
        early_index[...] = jnp.zeros_like(early_index)
        for number in range(early):
            found = find((2 + number) * plane, plane)
            early_index[2 * number : 2 * number + 2, :plane] = found[:2]

    placed = dot(placing[...], traces[...])
    own[...] = placed[: 2 * plane].astype(BF16)
    first = 2 * plane
    for part in parts:
        part[...] = placed[first : first + part.shape[0]].astype(BF16)
        first += part.shape[0]


def message_kernel(shots, shots_in, first, first_in, early_index, own_shot, out, level):
    terms = terms_of(shots, shots_in, first, first_in)
    level[...] = -select_rows(own_shot[...], terms)
    mean = jnp.sum(terms[:, :HALF], 1, keepdims=True) * (1 / HALF)
    high, low = halves(mean)
    out[:STATIONS, :] = (terms[:, :HALF] - mean).astype(BF16)
    lane = lax.broadcasted_iota(jnp.int32, (STATIONS, 128), 1)
    aux = jnp.where(lane == 0, terms[:, HALF : HALF + 1] - mean, 0.0)
    aux = jnp.where(lane == 1, high.astype(F32), jnp.where(lane == 2, low.astype(F32), aux))
    out[STATIONS : STATIONS + AUX, :] = jnp.transpose(aux)[:AUX].astype(BF16)
    out[STATIONS + AUX :, :] = early_index[...].astype(BF16)


def message_terms(message):
    aux = message[STATIONS : STATIONS + AUX, :].astype(F32)
    aux = jnp.transpose(jnp.concatenate([aux, jnp.zeros((128 - AUX, STATIONS), F32)], 0))
    mean = aux[:, 1:2] + aux[:, 2:3]
    return join(message[:STATIONS, :].astype(F32) + mean, aux[:, :] + mean)


def level_of(shot_row, shot_terms, receiver_row, receiver_terms):
    return -(
        select_rows(hot_rows(shot_row.astype(jnp.int32)), shot_terms)
        + select_rows(hot_rows(receiver_row.astype(jnp.int32)), receiver_terms)
    )


def put_gains(level, hilbert_high, hilbert_low, gains, at):
    first, second = halves(level)
    angle = (
        dot(first, hilbert_high[...])
        + dot(second, hilbert_high[...])
        + dot(first, hilbert_low[...])
    )
    sine, cosine = sin_cos(angle)
    size = jnp.exp(level[:, :HALF])
    real = size * cosine
    lane = lax.broadcasted_iota(jnp.int32, real.shape, 1)
    gains[0, at, :] = real
    gains[1, at, :] = size * sine
    gains[2, at, :] = jnp.where(lane == 0, jnp.exp(level[:, HALF : HALF + 1]), real)


def filter_block(block, forward, inverse, gains, before, at):
    spectra = dot(block, forward[...])
    real, imag = spectra[:, :HALF], spectra[:, HALF:]
    product = jnp.concatenate(
        [
            (real * gains[0, at, :] - imag * gains[1, at, :]).astype(BF16),
            (real * gains[1, at, :] + imag * gains[2, at, :]).astype(BF16),
        ],
        1,
    )
    series = dot(product, inverse[...])
    filtered = series[:, :HALF] + before[at, :]
    before[at, :] = series[:, HALF:]
    return filtered


def spans(width):
    return [slice(at, at + HALF) for at in range(0, width, HALF)]


def own_kernel(
    level, own_receiver, receivers, receivers_in, b, b_in,
    hilbert_high, hilbert_low, forward, inverse, traces, out, gains, before,
):
    rows = pl.ds(0, traces.shape[0])

    @pl.when(pl.program_id(0) == 0)
    def _():
        receiver_terms = terms_of(receivers, receivers_in, b, b_in)
        levels = level[...] - select_rows(own_receiver[...], receiver_terms)
        put_gains(levels[: traces.shape[0]], hilbert_high, hilbert_low, gains, rows)
        before[...] = jnp.zeros_like(before)

    for lanes in spans(traces.shape[1]):
        filtered = filter_block(traces[:, lanes], forward, inverse, gains, before, rows)
        out[:, lanes] = filtered.astype(BF16)


def relay_kernel(
    early, receivers, receivers_in, b, b_in, hilbert_high, hilbert_low, forward, inverse, *rest
):
    messages, parts = rest[:early], rest[early : early * (1 + PARTS)]
    outs, (gains, before, held) = rest[early * (1 + PARTS) : -3], rest[-3:]
    plane = held.shape[0] // early
    capacity = plane // len(outs)

    @pl.when(pl.program_id(0) == 0)
    def _():
        receiver_terms = terms_of(receivers, receivers_in, b, b_in)
        for number in range(early):
            message = messages[number]
            index = message[STATIONS + AUX :, :].astype(F32)[2 * number : 2 * number + 2]
            level = level_of(index[:1], message_terms(message), index[1:2], receiver_terms)
            at = pl.ds(number * plane, plane)
            put_gains(level[:plane], hilbert_high, hilbert_low, gains, at)
        before[...] = jnp.zeros_like(before)

    at = pl.ds(0, held.shape[0])
    for lanes in spans(held.shape[1]):
        block = jnp.concatenate([part[:, lanes] for part in parts], 0)
        held[:, lanes] = filter_block(block, forward, inverse, gains, before, at)
    for side, out in enumerate(outs):
        for number in range(early):
            first = number * plane + side * capacity
            out[number] = held[first : first + capacity, :].astype(BF16)


def gather_kernel(masks, sides, *refs):
    _, rcv = sides
    *got, out, sems = refs
    here, side = lax.axis_index("src"), lax.axis_index("rcv")
    copies = []
    for number, mask in enumerate(masks):
        for turn in range(rcv):
            place = (here ^ mask) * rcv + (side ^ turn)
            copies.append((got[turn].at[pl.ds(number, 1)], out.at[pl.ds(place, 1)]))
    copies = [pltpu.make_async_copy(*c, sems.at[i]) for i, c in enumerate(copies)]
    for copy in copies:
        copy.start()
    for copy in copies:
        copy.wait()


def finish_kernel(sides, _, late, out, sems):
    src, rcv = sides
    low = lax.axis_index("src") % (src // 2)
    copies = []
    for top in range(2):
        place = (top * (src // 2) + low) * rcv
        copies.append((late.at[pl.ds(top * rcv, rcv)], out.at[pl.ds(place, rcv)]))
    copies = [pltpu.make_async_copy(*c, sems.at[i]) for i, c in enumerate(copies)]
    for copy in copies:
        copy.start()
    for copy in copies:
        copy.wait()


def call(kernel, **options):
    params = pltpu.CompilerParams(vmem_limit_bytes=VMEM_LIMIT)
    return pl.pallas_call(kernel, compiler_params=params, **options)


def keep(*values, space=pltpu.VMEM):
    return tuple(pltpu.with_memory_space_constraint(value, space) for value in values)


def whole(shape):
    return pl.BlockSpec(shape, lambda *_: (0,) * len(shape))


def flip(value, name, mask):
    size = lax.axis_size(name)
    return lax.ppermute(value, name, [(i, i ^ mask) for i in range(size)])


def butterfly(value, name):
    other = jnp.zeros_like(value)
    bit, size = 1, lax.axis_size(name)
    while bit < size:
        if bit > 1:
            value = (value.astype(F32) + other.astype(F32)).astype(BF16)
        other = flip(value, name, bit)
        bit *= 2
    return value, other


def on_device(traces, trace_shot, trace_receiver, live, window_start, trace_owner):
    rows, samples = traces.shape
    src, rcv = lax.axis_size("src"), lax.axis_size("rcv")
    sides = (src, rcv)
    capacity = max(2, 3 * rows // (2 * src * rcv))
    plane = rcv * capacity
    masks = [mask for mask in range(1, src) if mask != src // 2]
    early = len(masks)
    (high, low), forward, inverse, (hilbert_high, hilbert_low) = tables()
    packed = jax.ShapeDtypeStruct((STATIONS + AUX, HALF), BF16)
    line = whole((1, rows))
    anywhere = pl.BlockSpec(memory_space=pltpu.HBM)
    inside = pl.BlockSpec(memory_space=pltpu.VMEM)
    block = min(128, rows)
    lines = [
        value.reshape(1, rows)
        for value in (trace_shot, trace_receiver, live, window_start, trace_owner)
    ]
    lines = keep(*lines, space=pltpu.HBM)
    shot, receiver, alive, _, owner = lines
    logs, shots, receivers = call(
        logs_kernel,
        grid=(rows // block,),
        in_specs=[line] * 4
        + [pl.BlockSpec((block, samples), lambda i: (i, 0)), whole((W, W)), whole((W, W))],
        out_specs=[whole((rows, WIDE)), whole(packed.shape), whole(packed.shape)],
        out_shape=[jax.ShapeDtypeStruct((rows, WIDE), F32), packed, packed])(*lines[:4], *keep(traces, high, low, space=pltpu.HBM))
    shots, shots_in = butterfly(shots, "rcv")
    receivers, receivers_in = butterfly(receivers, "src")

    def columns(size):
        return pl.BlockSpec((size, SPAN * HALF), lambda j: (0, j))

    def array(size):
        return jax.ShapeDtypeStruct((size, samples), BF16)

    own_lanes = pad_lanes(2 * plane)
    unit = plane // 16
    first, last = unit * SHARES[0] // 12 * 16, unit * SHARES[2] // 12 * 16
    sizes = [first, plane - first - last, last] * early
    own, *parts, own_shot, own_receiver, early_index = call(
        functools.partial(place_kernel, sides, capacity),
        grid=(samples // (SPAN * HALF),),
        in_specs=[line] * 3 + [columns(rows)],
        out_specs=[columns(2 * plane)]
        + [columns(size) for size in sizes]
        + [whole((own_lanes, STATIONS))] * 2
        + [whole((AUX, STATIONS))],
        out_shape=[array(2 * plane)]
        + [array(size) for size in sizes]
        + [jax.ShapeDtypeStruct((own_lanes, STATIONS), BF16)] * 2
        + [jax.ShapeDtypeStruct((AUX, STATIONS), F32)],
        scratch_shapes=[pltpu.VMEM((src * plane, rows), BF16)])(shot, receiver, owner, *keep(traces, space=pltpu.HBM))
    moved = []
    for number, part in enumerate(parts):
        moved.append(flip(part, "src", masks[number // PARTS]))
    firsts = keep(shots, shots_in, receivers, receivers_in)
    a, b = call(
        second_kernel,
        in_specs=[whole((1, rows))] * 3 + [whole((rows, WIDE))] + [inside] * 4,
        out_shape=[packed, packed])(
        shot, receiver, alive, logs, *firsts
    )
    a, a_in = butterfly(a, "rcv")
    b, b_in = butterfly(b, "src")
    seconds = keep(a, a_in, b, b_in)
    message, level = call(
        message_kernel,
        in_specs=[inside] * 4 + [whole(early_index.shape), whole(own_shot.shape)],
        out_shape=[
            jax.ShapeDtypeStruct((STATIONS + 2 * AUX, HALF), BF16),
            jax.ShapeDtypeStruct((own_lanes, WIDE), F32),
        ])(*seconds[:2], *firsts[:2], early_index, own_shot)
    messages = [flip(message, "src", mask) for mask in masks]
    sums = seconds + firsts
    shapes = [whole((WIDE, HALF)), whole((WIDE, HALF)), whole((HALF, W)), whole((W, W))]
    constants = (hilbert_high, hilbert_low, forward, inverse)
    ready = call(
        own_kernel,
        grid=(samples // (SPAN * HALF),),
        in_specs=[whole(level.shape), whole(own_receiver.shape)]
        + [inside] * 4
        + shapes
        + [columns(2 * plane)],
        out_specs=columns(2 * plane),
        out_shape=array(2 * plane),
        scratch_shapes=[
            pltpu.VMEM((3, 2 * plane, HALF), F32),
            pltpu.VMEM((2 * plane, HALF), F32),
        ])(level, own_receiver, *seconds[2:], *firsts[2:], *constants, own)
    groups = [
        [(low + top * (src // 2)) * rcv + side for top in range(2) for side in range(rcv)]
        for low in range(src // 2)
    ]
    late = lax.all_to_all(
        ready.reshape(2 * rcv, capacity, samples),
        ("src", "rcv"),
        split_axis=0,
        concat_axis=0,
        axis_index_groups=groups,
        tiled=True,
    )
    relayed = call(
        functools.partial(relay_kernel, early),
        grid=(samples // (SPAN * HALF),),
        in_specs=[inside] * 4
        + shapes
        + [inside] * early
        + [columns(size) for size in sizes],
        out_specs=[pl.BlockSpec((early, capacity, SPAN * HALF), lambda j: (0, 0, j))] * rcv,
        out_shape=[jax.ShapeDtypeStruct((early, capacity, samples), BF16)] * rcv,
        scratch_shapes=[
            pltpu.VMEM((3, early * plane, HALF), F32),
            pltpu.VMEM((early * plane, HALF), F32),
            pltpu.VMEM((early * plane, SPAN * HALF), F32),
        ])(*seconds[2:], *firsts[2:], *constants, *keep(*messages), *moved)
    got = [relayed[0]] + [flip(relayed[turn], "rcv", turn) for turn in range(1, rcv)]
    whole_out = jax.ShapeDtypeStruct((src * rcv, capacity, samples), BF16)
    half_done = call(
        functools.partial(gather_kernel, masks, sides),
        in_specs=[inside] * rcv,
        out_specs=anywhere,
        out_shape=whole_out,
        scratch_shapes=[pltpu.SemaphoreType.DMA((early * rcv,))])(*keep(*got))
    terms = jax.ShapeDtypeStruct((STATIONS, W), F32)
    shot_terms, receiver_terms = call(
        terms_kernel, in_specs=[inside] * 8, out_shape=[terms, terms])(*sums)
    regrouped = call(
        functools.partial(finish_kernel, sides),
        in_specs=[anywhere, inside],
        out_specs=anywhere,
        out_shape=whole_out,
        input_output_aliases={0: 0},
        scratch_shapes=[pltpu.SemaphoreType.DMA((2,))])(half_done, *keep(late))
    return (regrouped.reshape(src * plane, samples), shot_terms, receiver_terms)


def solution(mesh):
    return jax.shard_map(
        on_device,
        mesh=mesh,
        in_specs=(
            P(("src", "rcv"), None),
            P(("src", "rcv")),
            P(("src", "rcv")),
            P(("src", "rcv")),
            P(("src", "rcv")),
            P(("src", "rcv"), None),
        ),
        out_specs=(P(("src", "rcv"), None), P("src", None), P("rcv", None)),
        check_vma=False,
    )
```
